32 devices in a mesh: dp: 16 (over z, y, x), tensor: 2 (over core).
Axes of the slice: x: 2, y: 2, z: 4, core: 2. Of those that a mesh axis runs over, the one named last changes fastest.
Arguments:
- tokens: bfloat16 [32768, 768], P('dp'), may hold values from -6 to 6
- cotangent: bfloat16 [32768, 768], P('dp'), may hold values from -6 to 6
- seq_ids: int32 [32768], P('dp'), may hold values from 0 to 39, as said below
- block_slot: int32 [216], replicated, may hold values from 0 to 223, as said below
- masters: float32 [2, 224, 128, 128], P('tensor', 'dp')
- left_stats: float32 [2, 224, 128, 128], P('tensor', 'dp'), as said below
- right_stats: float32 [2, 224, 128, 128], P('tensor', 'dp'), as said below
- left_roots: float32 [2, 224, 128, 128], P('tensor', 'dp'), as said below
- right_roots: float32 [2, 224, 128, 128], P('tensor', 'dp'), as said below
- vectors: float32 [9984], replicated
- vector_momentum: float32 [9984], replicated, may hold values from -0.9 to 0.9
Outputs:
- mixed: bfloat16 [32768, 768], P(('dp', 'tensor'))
- input_grad: float32 [32768, 768], P(('dp', 'tensor'))
- matrix_grads: float32 [2, 224, 128, 128], P('tensor', 'dp')
- new_masters: float32 [2, 224, 128, 128], P('tensor', 'dp')
- new_left: float32 [2, 224, 128, 128], P('tensor', 'dp')
- new_right: float32 [2, 224, 128, 128], P('tensor', 'dp')
- new_vectors: float32 [9984], replicated
- new_vector_momentum: float32 [9984], replicated
The draws below stay inside these ranges and needn't reach their ends.
Inputs may be any that keep to these rules, and one draw needn't show every extreme that they name: `seq_ids`: each aligned block of 2048 tokens holds either one sequence or 4 sequences of 512 tokens, half of the blocks of each kind; ids count the sequences in order from 0 and are equal within a sequence. `block_slot`: Distinct; slot s belongs to index s // 14 of dp; slots that no block names hold no block. `left_stats`: symmetric in each slot. `right_stats`: symmetric in each slot. `left_roots`: symmetric in each slot. `right_roots`: symmetric in each slot.
All inputs are finite; a program needn't handle non-finite values.
Results may differ from the reference program's by a relative error of at most 0.0095.
Values may be sent and summed in bfloat16 or wider, within the bound.
No kernel may reach another device: no remote copies, remote signals or barrier semaphores. Data moves between devices by JAX's collectives and lax.ppermute only.
A program may use at most 256 MiB of HBM per device.

```python
import math
import jax
import jax.numpy as jnp
from jax import lax

D = 768
H = 12
HD = 64
ROT = 16
FF = 3072
BLK = 128
SHORT = 512
TOK_DEV = 2048
TENSOR_WAYS = 2
TOKENS = 32768
NBLK = 216
SLOT_ALL = 224
NVEC = 9984


def slot_order(key):
    shuffled = jax.random.permutation(jax.random.fold_in(key, 7), SLOT_ALL).astype(jnp.int32)
    where_top = jnp.argmax(shuffled == SLOT_ALL - 1)
    front_value = shuffled[0]
    settled = shuffled.at[where_top].set(front_value).at[0].set(SLOT_ALL - 1)
    return settled[:NBLK]


def draw_block_slot(key, part):
    return slot_order(key)


def draw_masters(key, part):
    chosen = slot_order(key)
    owner_of = jnp.full((SLOT_ALL,), NBLK, jnp.int32).at[chosen].set(jnp.arange(NBLK, dtype=jnp.int32))
    blocks_qkv = D // BLK * (3 * D // TENSOR_WAYS // BLK)
    blocks_attn = D // TENSOR_WAYS // BLK * (D // BLK)
    blocks_in = D // BLK * (FF // TENSOR_WAYS // BLK)
    base_scale = D ** (-0.5)
    spread = jnp.where(owner_of < blocks_qkv, base_scale, jnp.where(owner_of < blocks_qkv + blocks_attn, 4.0 * base_scale, jnp.where(owner_of < blocks_qkv + blocks_attn + blocks_in, base_scale, jnp.where(owner_of < NBLK, FF ** (-0.5), base_scale))))
    noise = jax.random.normal(jax.random.fold_in(key, 11), (TENSOR_WAYS, SLOT_ALL, BLK, BLK), jnp.float32)
    return noise * spread.astype(jnp.float32)[None, :, None, None]


def symmetric_draw(key, lowest, highest):
    factor = jnp.exp(jax.random.uniform(jax.random.fold_in(key, 3), (TENSOR_WAYS, SLOT_ALL, 1, 1), jnp.float32, math.log(lowest), math.log(highest)))
    raw_part = jax.random.normal(jax.random.fold_in(key, 5), (TENSOR_WAYS, SLOT_ALL, BLK, BLK), jnp.float32) * (0.21 / math.sqrt(BLK))
    identity = jnp.eye(BLK, dtype=jnp.float32)
    return factor * (identity + raw_part + jnp.swapaxes(raw_part, 2, 3))


def draw_left_stats(key, part):
    return symmetric_draw(jax.random.fold_in(key, 21), 0.1, 1.0)


def draw_right_stats(key, part):
    return symmetric_draw(jax.random.fold_in(key, 22), 0.1, 1.0)


def draw_left_roots(key, part):
    return symmetric_draw(jax.random.fold_in(key, 23), 0.5, 2.0)


def draw_right_roots(key, part):
    return symmetric_draw(jax.random.fold_in(key, 24), 0.5, 2.0)


def draw_vectors(key, part):
    normals = jax.random.normal(jax.random.fold_in(key, 31), (NVEC,), jnp.float32)
    gains = jax.random.uniform(jax.random.fold_in(key, 32), (NVEC,), jnp.float32, 0.6, 1.4)
    places = jnp.arange(NVEC, dtype=jnp.int32)
    is_gain = (places < D) | (places >= 2 * D) & (places < 3 * D)
    return jnp.where(is_gain, gains, 0.25 * normals)


def draw_seq_ids(key, part):
    shards = TOKENS // TOK_DEV
    per_block = TOK_DEV // SHORT
    kinds = jax.random.permutation(jax.random.fold_in(key, 41), shards).astype(jnp.int32) % 2
    counts = jnp.where(kinds == 1, per_block, 1).astype(jnp.int32)
    offsets = jnp.cumsum(counts) - counts
    within = jnp.arange(TOK_DEV, dtype=jnp.int32) // SHORT
    local_ids = jnp.where(kinds[:, None] == 1, within[None, :], 0)
    return (offsets[:, None] + local_ids).reshape(TOKENS).astype(jnp.int32)


def shard_levels(stream_key, dims, cuts, smallest, high):
    def one(dim, parts):
        heights = jax.random.uniform(jax.random.fold_in(jax.random.fold_in(stream_key, 6), dim), (parts,), jnp.float32, smallest / len(cuts), high / len(cuts))
        return jnp.repeat(jnp.exp(heights), dims[dim] // parts).reshape((-1,) + (1,) * (len(dims) - dim - 1))

    gain = one(*cuts[0])
    for cut in cuts[1:]:
        gain = gain * one(*cut)
    return gain


def centred(stream_key, dims, scale, reach, cuts=(), kind=jnp.bfloat16):
    drawn = scale * jax.random.normal(stream_key, dims, jnp.float32)
    if cuts:
        drawn = drawn * shard_levels(stream_key, dims, cuts, -0.22, 0.18)
    return jnp.clip(drawn, -reach, reach).astype(kind)


def setup_inputs(seed: int = 0) -> dict:
    keys = jax.random.split(jax.random.key(seed), 12)
    tokens = centred(keys[0], (TOKENS, D), 1.0, 6.0, ((0, 16),))
    cotangent = centred(keys[1], (TOKENS, D), 1.0, 6.0, ((0, 16),))
    seq_ids = draw_seq_ids(jax.random.fold_in(keys[11], 71), 0)
    block_slot = draw_block_slot(jax.random.fold_in(keys[11], 71), 0)
    masters = draw_masters(jax.random.fold_in(keys[11], 71), 0)
    left_stats = draw_left_stats(jax.random.fold_in(keys[11], 71), 0)
    right_stats = draw_right_stats(jax.random.fold_in(keys[11], 71), 0)
    left_roots = draw_left_roots(jax.random.fold_in(keys[11], 71), 0)
    right_roots = draw_right_roots(jax.random.fold_in(keys[11], 71), 0)
    vectors = draw_vectors(jax.random.fold_in(keys[11], 71), 0)
    vector_momentum = centred(keys[10], (NVEC,), 0.15, 0.9, (), jnp.float32)
    return {"tokens": tokens, "cotangent": cotangent, "seq_ids": seq_ids, "block_slot": block_slot, "masters": masters, "left_stats": left_stats, "right_stats": right_stats, "left_roots": left_roots, "right_roots": right_roots, "vectors": vectors, "vector_momentum": vector_momentum}


@jax.custom_vjp
def low(v):
    return lax.optimization_barrier(v.astype(jnp.bfloat16)).astype(jnp.float32)

@jax.custom_vjp
def low_back(v):
    return v

def low_keep(v):
    return (low(v), None)

def low_pass(kept, grad):
    return (grad,)

def back_keep(v):
    return (v, None)

def back_low(kept, grad):
    return (low(grad),)
low.defvjp(low_keep, low_pass)
low_back.defvjp(back_keep, back_low)
norm_eps = 1e-05
floor_score = -1e+30

def matmul_high(first_op, second_op):
    return jnp.dot(first_op, second_op, precision=lax.Precision.HIGHEST, preferred_element_type=jnp.float32)

def unblock(blocks, row_total, col_total):
    return blocks.reshape(row_total // BLK, col_total // BLK, BLK, BLK).transpose(0, 2, 1, 3).reshape(row_total, col_total)

def to_blocks(matrix):
    row_count, col_count = matrix.shape
    return matrix.reshape(row_count // BLK, BLK, col_count // BLK, BLK).transpose(0, 2, 1, 3).reshape(-1, BLK, BLK)

def rotate(values, cosine_tab, sine_tab, local_heads):
    tok_rows = values.shape[0]
    shaped = values.reshape(tok_rows, local_heads, HD)
    rot_half = ROT // 2
    lower_half = shaped[:, :, :rot_half]
    upper_half = shaped[:, :, rot_half:ROT]
    turned = jnp.concatenate([lower_half * cosine_tab - upper_half * sine_tab, upper_half * cosine_tab + lower_half * sine_tab, shaped[:, :, ROT:]], axis=2)
    return turned.reshape(tok_rows, local_heads * HD)

def shard_attention(pieces):
    queries, keys_rot, values_all, ids_shard = pieces
    order = jnp.arange(TOK_DEV, dtype=jnp.int32)
    score_scale = HD ** (-0.5)
    scores = jnp.einsum('qhe,khe->hqk', queries, keys_rot, precision=lax.Precision.HIGHEST) * score_scale
    allowed = (ids_shard[:, None] == ids_shard[None, :]) & (order[:, None] >= order[None, :])
    scores = low_back(jnp.where(allowed[None], scores, floor_score))
    row_max = lax.optimization_barrier(jnp.max(scores, axis=2, keepdims=True))
    exp_scores = jnp.exp(scores - row_max)
    weights_low = low(exp_scores / lax.optimization_barrier(jnp.sum(exp_scores, axis=2, keepdims=True)))
    return jnp.einsum('hqk,khe->qhe', weights_low, values_all, precision=lax.Precision.HIGHEST)

def reference(tokens, cotangent, seq_ids, block_slot, masters, left_stats, right_stats, left_roots, right_roots, vectors, vector_momentum):
    local_heads = H // TENSOR_WAYS
    width_qkv = 3 * D // TENSOR_WAYS
    width_heads = D // TENSOR_WAYS
    width_hidden = FF // TENSOR_WAYS
    blocks_qkv = D // BLK * (width_qkv // BLK)
    blocks_attn = width_heads // BLK * (D // BLK)
    blocks_in = D // BLK * (width_hidden // BLK)
    copies = masters.astype(jnp.bfloat16).astype(jnp.float32)
    picked = copies[:, block_slot]
    mark_one = blocks_qkv
    mark_two = blocks_qkv + blocks_attn
    mark_three = mark_two + blocks_in
    w_qkv = jnp.stack([unblock(picked[shard_index, :mark_one], D, width_qkv) for shard_index in range(TENSOR_WAYS)])
    w_attn = jnp.stack([unblock(picked[shard_index, mark_one:mark_two], width_heads, D) for shard_index in range(TENSOR_WAYS)])
    w_in = jnp.stack([unblock(picked[shard_index, mark_two:mark_three], D, width_hidden) for shard_index in range(TENSOR_WAYS)])
    w_out = jnp.stack([unblock(picked[shard_index, mark_three:], width_hidden, D) for shard_index in range(TENSOR_WAYS)])
    shards = TOKENS // TOK_DEV
    places = jnp.arange(TOK_DEV, dtype=jnp.int32)
    ids_grid = seq_ids.reshape(shards, TOK_DEV)
    seq_first = jnp.concatenate([jnp.broadcast_to(places[:1] == 0, (shards, 1)), ids_grid[:, 1:] != ids_grid[:, :-1]], axis=1)
    seq_start = lax.cummax(jnp.where(seq_first, places[None, :], 0), axis=1)
    position = (places[None, :] - seq_start).reshape(TOKENS).astype(jnp.float32)
    rot_half = ROT // 2
    inverse = 10000.0 ** (-(2.0 * jnp.arange(rot_half, dtype=jnp.float32)) / ROT)
    angles = position[:, None] * inverse[None, :]
    cosine_tab = jnp.cos(angles)[:, None, :]
    sine_tab = jnp.sin(angles)[:, None, :]

    def grid_heads(values):
        return values.reshape(shards, TOK_DEV, local_heads, HD)

    def forward(w_qkv, w_attn, w_in, w_out, vector_all, tokens_f):
        row_mean = lax.optimization_barrier(jnp.mean(tokens_f, axis=1, keepdims=True))
        centered = tokens_f - row_mean
        inv_std = lax.rsqrt(lax.optimization_barrier(jnp.mean(centered * centered, axis=1, keepdims=True)) + norm_eps)
        normed = centered * inv_std
        norm_one = low(normed * vector_all[0:D] + vector_all[D:2 * D])
        norm_two = low(normed * vector_all[2 * D:3 * D] + vector_all[3 * D:4 * D])
        result = tokens_f + vector_all[7 * D:8 * D] + vector_all[8 * D + FF:9 * D + FF]
        for shard_index in range(TENSOR_WAYS):
            bias_qkv = vector_all[4 * D + shard_index * width_qkv:4 * D + (shard_index + 1) * width_qkv]
            mixed_qkv = low_back(matmul_high(norm_one, w_qkv[shard_index]) + bias_qkv)
            queries = low(rotate(mixed_qkv[:, :width_heads], cosine_tab, sine_tab, local_heads))
            keys_rot = low(rotate(mixed_qkv[:, width_heads:2 * width_heads], cosine_tab, sine_tab, local_heads))
            values_all = low(mixed_qkv[:, 2 * width_heads:])
            attended = lax.map(jax.checkpoint(shard_attention), (grid_heads(queries), grid_heads(keys_rot), grid_heads(values_all), ids_grid))
            attended = low(low_back(attended.reshape(TOKENS, width_heads)))
            bias_in = vector_all[8 * D + shard_index * width_hidden:8 * D + (shard_index + 1) * width_hidden]
            pre_hidden = low_back(matmul_high(norm_two, w_in[shard_index]) + bias_in)
            hidden = low(jax.nn.gelu(pre_hidden, approximate=False))
            result = result + matmul_high(attended, w_attn[shard_index]) + matmul_high(hidden, w_out[shard_index])
        return result
    tokens_f = tokens.astype(jnp.float32)
    output, pullback = jax.vjp(forward, w_qkv, w_attn, w_in, w_out, vectors, tokens_f)
    grad_qkv, grad_attn, grad_in, grad_out, grad_vec, input_grad = pullback(cotangent.astype(jnp.float32))
    grad_scale = 1.0 / jnp.sqrt(jnp.float32(TOKENS))
    block_grads = jnp.stack([jnp.concatenate([to_blocks(grad_qkv[shard_index]), to_blocks(grad_attn[shard_index]), to_blocks(grad_in[shard_index]), to_blocks(grad_out[shard_index])], axis=0) for shard_index in range(TENSOR_WAYS)]) * grad_scale
    matrix_grads = jnp.zeros((TENSOR_WAYS, SLOT_ALL, BLK, BLK), jnp.float32).at[:, block_slot].set(block_grads)
    highest = lax.Precision.HIGHEST
    new_left = 0.5 * left_stats + 0.5 * jnp.einsum('tsij,tskj->tsik', matrix_grads, matrix_grads, precision=highest) / BLK
    new_right = 0.5 * right_stats + 0.5 * jnp.einsum('tsji,tsjk->tsik', matrix_grads, matrix_grads, precision=highest) / BLK
    update_step = jnp.einsum('tsij,tsjk->tsik', left_roots, matrix_grads, precision=highest)
    update_step = jnp.einsum('tsij,tsjk->tsik', update_step, right_roots, precision=highest)
    new_masters = masters - 0.03 * update_step
    vector_grad = grad_vec * grad_scale
    new_momentum = 0.9 * vector_momentum + 0.1 * vector_grad
    new_vectors = vectors - 1.5 * new_momentum
    return (output.astype(jnp.bfloat16), input_grad, matrix_grads, new_masters, new_left, new_right, new_vectors, new_momentum)
```

```python
import functools

import jax
import jax.numpy as jnp
import numpy as np
from jax import lax
from jax.experimental import pallas as pl
from jax.experimental.pallas import tpu as pltpu
from jax.sharding import PartitionSpec as P

H = 12
HD = 64
ROT = 16
FF = 3072

norm_eps = 1e-05
floor_score = -1e30
rate_matrix = 0.03
rate_vector = 1.5
decay_vector = 0.9

BF = jnp.bfloat16
F32 = jnp.float32
TILE = 512
ANY = pl.BlockSpec(memory_space=pl.ANY)


def dot(a, b, ca=1, cb=0):
    return lax.dot_general(a, b, (((ca,), (cb,)), ((), ())), preferred_element_type=F32)


def row_spec(width, rows=TILE):
    return pl.BlockSpec((rows, width), lambda i, *_: (i, 0))


def col_spec(height, cols=TILE):
    return pl.BlockSpec((height, cols), lambda i, *_: (0, i))


def full_spec(shape):
    return pl.BlockSpec(shape, lambda *_: (0,) * len(shape))


def params(**kw):
    return pltpu.CompilerParams(vmem_limit_bytes=60 << 20, **kw)


def code_of(mat, row, col):
    return (mat << 16) | (row << 8) | col


def load_blocks(table, arrays, targets, sem):
    base = 0
    for array in arrays:
        count, blk, _ = array.shape

        def body(p, carry, array=array, base=base, blk=blk):
            code = table[base + p]
            mat = code >> 16
            row = pl.multiple_of(((code >> 8) & 255) * blk, blk)
            col = pl.multiple_of((code & 255) * blk, blk)
            for which, ref in targets:

                @pl.when(mat == which)
                def _(ref=ref):
                    pltpu.make_async_copy(
                        array.at[p], ref.at[pl.ds(row, blk), pl.ds(col, blk)], sem
                    ).start()

            return carry

        lax.fori_loop(0, count, body, 0)
        base += count
    for _, ref in targets:
        pltpu.make_async_copy(ref, ref, sem).wait()


def store_blocks(table, arrays, sources, sem):
    base = 0
    for array in arrays:
        count, blk, _ = array.shape

        def body(p, carry, array=array, base=base, blk=blk):
            code = table[base + p]
            mat = code >> 16
            row = pl.multiple_of(((code >> 8) & 255) * blk, blk)
            col = pl.multiple_of((code & 255) * blk, blk)
            for which, ref in sources:

                @pl.when(mat == which)
                def _(ref=ref):
                    pltpu.make_async_copy(
                        ref.at[pl.ds(row, blk), pl.ds(col, blk)], array.at[p], sem
                    ).start()

            return carry

        lax.fori_loop(0, count, body, 0)
        base += count
    for _, ref in sources:
        pltpu.make_async_copy(ref, ref, sem).wait()


def turn(v, cos, low, high):
    half = ROT // 2
    lanes = v.shape[-1]
    return v * cos + pltpu.roll(v, lanes - half, 1) * low + pltpu.roll(v, half, 1) * high


def project_kernel(n_arr, table, *refs):
    arrays = refs[:n_arr]
    n1, dy, bias, cos, low, high, q_o, k_o, v_o, da_o, wa, wo, sem = refs[n_arr:]

    @pl.when(pl.program_id(0) == 0)
    def _():
        load_blocks(table, arrays, ((0, wa), (1, wo)), sem)

    z = dot(n1[...], wa[...]) + bias[...]
    width = wo.shape[0]
    c, lo, hi = cos[...], low[...], high[...]
    for g in range(width // 128):
        part = z[:, g * 128 : (g + 1) * 128]
        q_o[:, g * 128 : (g + 1) * 128] = (turn(part, c, lo, hi) * (HD**-0.5)).astype(BF)
        part = z[:, width + g * 128 : width + (g + 1) * 128]
        k_o[:, g * 128 : (g + 1) * 128] = turn(part, c, lo, hi).astype(BF)
    v_o[...] = z[:, 2 * width :].astype(BF)
    da_o[...] = dot(dy[...], wo[...], 1, 1)


def project(table, arrays, n1, dy, bias, tabs, width):
    rows, dim = n1.shape
    spec = pltpu.PrefetchScalarGridSpec(
        num_scalar_prefetch=1,
        grid=(rows // TILE,),
        in_specs=[ANY] * len(arrays)
        + [row_spec(dim), row_spec(dim), full_spec(bias.shape)]
        + [row_spec(128)] * 3,
        out_specs=[row_spec(width)] * 4,
        scratch_shapes=[
            pltpu.VMEM((dim, 3 * width), BF),
            pltpu.VMEM((width, dim), BF),
            pltpu.SemaphoreType.DMA,
        ],
    )
    return pl.pallas_call(
        functools.partial(project_kernel, len(arrays)),
        grid_spec=spec,
        out_shape=[jax.ShapeDtypeStruct((rows, width), BF)] * 3
        + [jax.ShapeDtypeStruct((rows, width), F32)],
        compiler_params=params(),
        name="project",
    )(table, *arrays, n1, dy, bias, *tabs)


def attend_kernel(single, q, k, v, da, cos, low, high, a_o, dq_o, dk_o, dv_o, s_sc, p_sc, dk_sc, dv_sc):
    i = pl.program_id(1)
    blk = q.shape[0]
    first = lax.broadcasted_iota(jnp.int32, (1, 128), 1) < HD
    sel = (first.astype(F32), 1.0 - first.astype(F32))

    @pl.when(i == 0)
    def _():
        dk_sc[...] = jnp.zeros_like(dk_sc)
        dv_sc[...] = jnp.zeros_like(dv_sc)

    start = jnp.where(single[0] == 1, 0, i)
    q_f = q[...].astype(F32)
    qs = [(q_f * m).astype(BF) for m in sel]

    def lanes(x, op):
        out = x[:, :128]
        for g in range(1, x.shape[1] // 128):
            out = op(out, x[:, g * 128 : (g + 1) * 128])
        return out

    def rows_of(ref, j):
        return ref[pl.ds(pl.multiple_of(j * blk, blk), blk), :]

    def score(j, carry, diagonal=False):
        kj = rows_of(k, j)
        cols = pl.ds(pl.multiple_of(j * blk, blk), blk)
        out = []
        for h in range(2):
            s = dot(qs[h], kj, 1, 1)
            if diagonal:
                r = lax.broadcasted_iota(jnp.int32, s.shape, 0)
                c = lax.broadcasted_iota(jnp.int32, s.shape, 1)
                s = jnp.where(r >= c, s, floor_score)
            s_sc[h, :, cols] = s
            out.append(jnp.maximum(carry[h], lanes(s, jnp.maximum)))
        return tuple(out)

    lowest = jnp.full((blk, 128), floor_score, F32)
    tops = lax.fori_loop(start, i, score, (lowest, lowest))
    tops = score(i, tops, True)
    tops = [jnp.max(t, axis=1, keepdims=True) for t in tops]

    def weigh(j, carry):
        sums, acc = carry
        vj = rows_of(v, j).astype(F32)
        cols = pl.ds(pl.multiple_of(j * blk, blk), blk)
        out = []
        for h in range(2):
            p = jnp.exp(s_sc[h, :, cols] - tops[h])
            out.append(sums[h] + lanes(p, jnp.add))
            pb = p.astype(BF)
            p_sc[h, :, cols] = pb
            acc = acc + dot(pb, (vj * sel[h]).astype(BF))
        return tuple(out), acc

    zero = jnp.zeros((blk, 128), F32)
    sums, acc = lax.fori_loop(start, i + 1, weigh, ((zero, zero), zero))
    invs = [1.0 / jnp.sum(t, axis=1, keepdims=True) for t in sums]
    inv = invs[0] * sel[0] + invs[1] * sel[1]
    a = acc * inv
    a_o[...] = a.astype(BF)
    das = [(da[...] * inv * m).astype(BF) for m in sel]
    deltas = [jnp.sum(d.astype(F32) * a, axis=1, keepdims=True) for d in das]

    def back(j, dq):
        at = pl.ds(pl.multiple_of(j * blk, blk), blk)
        kj, vj = k[at, :], v[at, :]
        kf = kj.astype(F32)
        dk, dv = dk_sc[at, :], dv_sc[at, :]
        for h in range(2):
            pb = p_sc[h, :, at]
            dp = dot(das[h], vj, 1, 1)
            ds = (pb.astype(F32) * (dp - deltas[h])).astype(BF)
            dq = dq + dot(ds, (kf * sel[h]).astype(BF))
            dk = dk + dot(ds, qs[h], 0, 0)
            dv = dv + dot(pb, das[h], 0, 0)
        dk_sc[at, :] = dk
        dv_sc[at, :] = dv
        return dq

    dq = lax.fori_loop(start, i + 1, back, zero)
    at = pl.ds(pl.multiple_of(i * blk, blk), blk)
    dq_o[...] = turn(dq * (HD**-0.5), cos[at, :], -low[at, :], -high[at, :]).astype(BF)

    @pl.when(i == pl.num_programs(1) - 1)
    def _():
        dk_o[...] = turn(dk_sc[...], cos[...], -low[...], -high[...]).astype(BF)
        dv_o[...] = dv_sc[...].astype(BF)


def attend(single, q, k, v, da, tabs):
    rows, width = q.shape
    blk = min(TILE, rows)
    tile = pl.BlockSpec((blk, 128), lambda h, i, *_: (i, h))
    whole = pl.BlockSpec((rows, 128), lambda h, i, *_: (0, h))
    table = pl.BlockSpec((rows, 128), lambda h, i, *_: (0, 0))
    spec = pltpu.PrefetchScalarGridSpec(
        num_scalar_prefetch=1,
        grid=(width // 128, rows // blk),
        in_specs=[tile, whole, whole, tile, table, table, table],
        out_specs=[tile, tile, whole, whole],
        scratch_shapes=[
            pltpu.VMEM((2, blk, rows), F32),
            pltpu.VMEM((2, blk, rows), BF),
            pltpu.VMEM((rows, 128), F32),
            pltpu.VMEM((rows, 128), F32),
        ],
    )
    return pl.pallas_call(
        attend_kernel,
        grid_spec=spec,
        out_shape=[jax.ShapeDtypeStruct((rows, width), BF)] * 4,
        compiler_params=params(),
        name="attend",
    )(single, q, k, v, da, *tabs)


def gelu_parts(u):
    cdf = 0.5 * (1.0 + lax.erf(u * 0.7071067811865476))
    return cdf, jnp.exp(-0.5 * u * u) * 0.3989422804014327


def feed_kernel(n_arr, n_out, table, where_to, *refs):
    arrays = refs[:n_arr]
    n2, n2t, dy, dyt, bias = refs[n_arr : n_arr + 5]
    out_o, dn2_o, db_o = refs[n_arr + 5 : n_arr + 8]
    sends = refs[n_arr + 8 : n_arr + 8 + n_out]
    wi, wu, di, dut, stage_i, stage_u, sem = refs[n_arr + 8 + n_out :]
    step = pl.program_id(0)

    @pl.when(step == 0)
    def _():
        load_blocks(table, arrays, ((2, wi), (3, wu)), sem)
        di[...] = jnp.zeros_like(di)
        dut[...] = jnp.zeros_like(dut)
        db_o[...] = jnp.zeros_like(db_o)

    hidden = wi.shape[1]
    part = 512
    x, xt, g, gt = n2[...], n2t[...], dy[...], dyt[...]
    for j in range(hidden // part):
        at = pl.ds(j * part, part)
        hp = dot(x, wi[:, at]) + bias[:, at]
        dh = dot(g, wu[at, :], 1, 1)
        cdf, dens = gelu_parts(hp)
        hb = (hp * cdf).astype(BF)
        dh = (dh * (cdf + hp * dens)).astype(BF)
        db_o[:, at] += jnp.sum(dh.astype(F32), axis=0, keepdims=True)
        o = dot(hb, wu[at, :])
        d = dot(dh, wi[:, at], 1, 1)
        if j == 0:
            out_o[...] = o
            dn2_o[...] = d
        else:
            out_o[...] += o
            dn2_o[...] += d
        di[:, at] += dot(xt, dh)
        dut[:, at] += dot(gt, hb)

    @pl.when(step == pl.num_programs(0) - 1)
    def _():
        stage_i[...] = di[...].astype(BF)
        for j in range(hidden // 128):
            stage_u[j * 128 : (j + 1) * 128, :] = dut[:, j * 128 : (j + 1) * 128].T.astype(BF)
        store_blocks(where_to, sends, ((2, stage_i), (3, stage_u)), sem)


def feed(table, where_to, arrays, n2, n2t, dy, dyt, bias, send_shapes):
    rows, dim = n2.shape
    hidden = bias.shape[1]
    spec = pltpu.PrefetchScalarGridSpec(
        num_scalar_prefetch=2,
        grid=(rows // TILE,),
        in_specs=[ANY] * len(arrays)
        + [row_spec(dim), col_spec(dim), row_spec(dim), col_spec(dim), full_spec(bias.shape)],
        out_specs=[row_spec(dim), row_spec(dim), full_spec(bias.shape)] + [ANY] * len(send_shapes),
        scratch_shapes=[
            pltpu.VMEM((dim, hidden), BF),
            pltpu.VMEM((hidden, dim), BF),
            pltpu.VMEM((dim, hidden), F32),
            pltpu.VMEM((dim, hidden), F32),
            pltpu.VMEM((dim, hidden), BF),
            pltpu.VMEM((hidden, dim), BF),
            pltpu.SemaphoreType.DMA,
        ],
    )
    out = pl.pallas_call(
        functools.partial(feed_kernel, len(arrays), len(send_shapes)),
        grid_spec=spec,
        out_shape=[jax.ShapeDtypeStruct((rows, dim), F32)] * 2
        + [jax.ShapeDtypeStruct(bias.shape, F32)]
        + send_shapes,
        compiler_params=params(),
        name="feed",
    )(table, where_to, *arrays, n2, n2t, dy, dyt, bias)
    return out[0], out[1], out[2], out[3:]


def close_kernel(n_arr, n_out, table, where_to, order, *refs):
    arrays = refs[:n_arr]
    refs = refs[n_arr + n_out :]
    n1t, dq, dk, dv, a, dyt, x, mean, inv, dn2, ffn, gains = refs[:12]
    own_mix, far_mix, own_in, far_in, sums, db_o = refs[12:18]
    sends = refs[18 : 18 + n_out]
    wa, wo, dwa, dot_, stage_a, stage_o, sem = refs[18 + n_out :]
    step = pl.program_id(0)
    steps = pl.num_programs(0)

    @pl.when(step == 0)
    def _():
        load_blocks(table, arrays, ((0, wa), (1, wo)), sem)
        dwa[...] = jnp.zeros_like(dwa)
        dot_[...] = jnp.zeros_like(dot_)
        sums[...] = jnp.zeros_like(sums)
        db_o[...] = jnp.zeros_like(db_o)

    width = wo.shape[0]
    n1, parts = n1t[...], (dq[...], dk[...], dv[...])
    dn1 = None
    for g, dz in enumerate(parts):
        at = pl.ds(g * width, width)
        d = dot(dz, wa[:, at], 1, 1)
        dn1 = d if dn1 is None else dn1 + d
        dwa[:, at] += dot(n1, dz)
        db_o[:, at] += jnp.sum(dz.astype(F32), axis=0, keepdims=True)
    dot_[...] += dot(dyt[...], a[...])
    mix = (dot(a[...], wo[...]) + ffn[...]).astype(BF)
    hat = (x[...].astype(F32) - mean[...]) * inv[...]
    d2 = dn2[...]
    sums[0:1, :] += jnp.sum(dn1 * hat, axis=0, keepdims=True)
    sums[1:2, :] += jnp.sum(dn1, axis=0, keepdims=True)
    sums[2:3, :] += jnp.sum(d2 * hat, axis=0, keepdims=True)
    sums[3:4, :] += jnp.sum(d2, axis=0, keepdims=True)
    d = dn1 * gains[0:1, :] + d2 * gains[1:2, :]
    scale = 1.0 / d.shape[1]
    d_mean = jnp.sum(d, axis=1, keepdims=True) * scale
    d_hat = jnp.sum(d * hat, axis=1, keepdims=True) * scale
    back = ((d - d_mean - hat * d_hat) * inv[...]).astype(BF)

    @pl.when(step < steps // 2)
    def _():
        far_mix[...] = mix
        far_in[...] = back

    @pl.when(step >= steps // 2)
    def _():
        own_mix[...] = mix
        own_in[...] = back

    @pl.when(step == steps - 1)
    def _():
        stage_a[...] = dwa[...].astype(BF)
        for j in range(width // 128):
            stage_o[j * 128 : (j + 1) * 128, :] = dot_[:, j * 128 : (j + 1) * 128].T.astype(BF)
        store_blocks(where_to, sends, ((0, stage_a), (1, stage_o)), sem)


def close(table, where_to, order, arrays, sends, n1t, dq, dk, dv, a, dyt, x, mean, inv, dn2, ffn, gains):
    rows, dim = x.shape
    width = a.shape[1]
    steps = rows // TILE
    half = steps // 2

    def tile(w):
        return pl.BlockSpec((TILE, w), lambda i, t, s, o: (o[i], 0))

    def tile_t(h):
        return pl.BlockSpec((h, TILE), lambda i, t, s, o: (0, o[i]))

    far = pl.BlockSpec((TILE, dim), lambda i, *_: (jnp.minimum(i, half - 1), 0))
    own = pl.BlockSpec((TILE, dim), lambda i, *_: (jnp.maximum(i - half, 0), 0))
    n_arr, n_out = len(arrays), len(sends)
    spec = pltpu.PrefetchScalarGridSpec(
        num_scalar_prefetch=3,
        grid=(steps,),
        in_specs=[ANY] * (n_arr + n_out)
        + [tile_t(dim)]
        + [tile(width)] * 4
        + [tile_t(dim), tile(dim), tile(1), tile(1), tile(dim), tile(dim), full_spec(gains.shape)],
        out_specs=[own, far, own, far, full_spec((8, dim)), full_spec((1, 3 * width))] + [ANY] * n_out,
        scratch_shapes=[
            pltpu.VMEM((dim, 3 * width), BF),
            pltpu.VMEM((width, dim), BF),
            pltpu.VMEM((dim, 3 * width), F32),
            pltpu.VMEM((dim, width), F32),
            pltpu.VMEM((dim, 3 * width), BF),
            pltpu.VMEM((width, dim), BF),
            pltpu.SemaphoreType.DMA,
        ],
    )
    half_shape = jax.ShapeDtypeStruct((rows // 2, dim), BF)
    out = pl.pallas_call(
        functools.partial(close_kernel, n_arr, n_out),
        grid_spec=spec,
        out_shape=[half_shape] * 4
        + [jax.ShapeDtypeStruct((8, dim), F32), jax.ShapeDtypeStruct((1, 3 * width), F32)]
        + [jax.ShapeDtypeStruct(s.shape, s.dtype) for s in sends],
        input_output_aliases={3 + n_arr + i: 6 + i for i in range(n_out)},
        compiler_params=params(),
        name="close",
    )(table, where_to, order, *arrays, *sends, n1t, dq, dk, dv, a, dyt, x, mean, inv, dn2, ffn, gains)
    return out[:6], out[6:]


def own_kernel(n_part, valid, *refs):
    parts = refs[:n_part]
    masters, left, right, root_l, root_r = refs[n_part : n_part + 5]
    grad_o, master_o, left_o, right_o = refs[n_part + 5 :]
    s = pl.program_id(0)
    g = parts[0][0].astype(F32)
    for p in parts[1:]:
        g = g + p[0].astype(F32)
    scale = valid[s]
    blk = g.shape[0]
    g = jnp.where(scale > 0, g * scale, 0.0)
    hi = lax.Precision.HIGHEST
    dims = lambda a, b: (((a,), (b,)), ((), ()))
    dg = lambda p, q, a, b: lax.dot_general(p, q, dims(a, b), precision=hi, preferred_element_type=F32)
    grad_o[0] = g
    left_o[0] = 0.5 * left[0] + (0.5 / blk) * dg(g, g, 1, 1)
    right_o[0] = 0.5 * right[0] + (0.5 / blk) * dg(g, g, 0, 0)
    master_o[0] = masters[0] - rate_matrix * dg(dg(root_l[0], g, 1, 0), root_r[0], 1, 0)


def own_update(valid, parts, masters, left, right, root_l, root_r):
    count, blk, _ = masters.shape
    one = pl.BlockSpec((1, blk, blk), lambda s, *_: (s, 0, 0))
    spec = pltpu.PrefetchScalarGridSpec(
        num_scalar_prefetch=1,
        grid=(count,),
        in_specs=[one] * (len(parts) + 5),
        out_specs=[one] * 4,
    )
    return pl.pallas_call(
        functools.partial(own_kernel, len(parts)),
        grid_spec=spec,
        out_shape=[jax.ShapeDtypeStruct(masters.shape, F32)] * 4,
        compiler_params=params(),
        name="own_update",
    )(valid, *parts, masters, left, right, root_l, root_r)


class Plan:
    def __init__(self, data_ways, slot_count):
        self.data_ways = data_ways
        self.slots = slot_count
        self.fast = data_ways == 16
        if self.fast:
            base, extra = divmod(slot_count, min(4, slot_count))
            sizes = [base + (i < extra) for i in range(min(4, slot_count))]
            self.chunks = []
            at = 0
            for size in sizes:
                self.chunks.append((at, size))
                at += size
            self.px = [(i, i ^ 1) for i in range(16)]
            self.py = [(i, i ^ 2) for i in range(16)]
            self.pz = [[(i, (i + 4 * d) % 16) for i in range(16)] for d in range(4)]

    def gather(self, copies):
        if not self.fast:
            return [lax.all_gather(copies, "dp", axis=0, tiled=True)]
        stages = []
        for at, size in self.chunks:
            mine = copies[at : at + size]
            line = [mine] + [lax.ppermute(mine, "dp", self.pz[d]) for d in range(1, 4)]
            stages.append(jnp.concatenate(line, axis=0))
        out = []
        for c, line in enumerate(stages):
            x1 = lax.ppermute(line, "dp", self.px)
            y1 = lax.ppermute(line, "dp", self.py)
            if c % 2 == 0:
                xy = lax.ppermute(x1, "dp", self.py)
            else:
                xy = lax.ppermute(y1, "dp", self.px)
            out += [line, x1, y1, xy]
        return out

    def positions(self, index, sign):
        if not self.fast:
            return jnp.arange(self.data_ways * self.slots, dtype=jnp.int32)
        z, y, x = index // 4, (index // 2) % 2, index % 2
        rel = []
        for at, size in self.chunks:
            for yr, xr in ((0, 0), (0, 1), (1, 0), (1, 1)):
                for zr in range(4):
                    for j in range(size):
                        rel.append((zr, yr, xr, at + j))
        rel = np.array(rel, np.int32)
        owner = ((z + sign * rel[:, 0]) % 4) * 4 + (y ^ rel[:, 1]) * 2 + (x ^ rel[:, 2])
        return owner * self.slots + rel[:, 3]

    def send_shapes(self, blk):
        if not self.fast:
            return [jax.ShapeDtypeStruct((self.data_ways * self.slots, blk, blk), BF)]
        return [jax.ShapeDtypeStruct((4 * size, blk, blk), BF) for _, size in self.chunks for _ in range(4)]

    def scatter(self, sends):
        if not self.fast:
            return [lax.psum_scatter(sends[0], "dp", scatter_dimension=0, tiled=True)]

        def add(*parts):
            total = parts[0].astype(F32)
            for p in parts[1:]:
                total = total + p.astype(F32)
            return total.astype(BF)

        parts = [[] for _ in range(4)]
        for c, (at, size) in enumerate(self.chunks):
            own, xs, ys, xy = sends[4 * c : 4 * c + 4]
            if c % 2 == 0:
                xs = add(xs, lax.ppermute(xy, "dp", self.py))
            else:
                ys = add(ys, lax.ppermute(xy, "dp", self.px))
            own = add(own, lax.ppermute(xs, "dp", self.px), lax.ppermute(ys, "dp", self.py))
            parts[0].append(own[:size])
            for d in range(1, 4):
                parts[d].append(lax.ppermute(own[d * size : (d + 1) * size], "dp", self.pz[d]))
        return [jnp.concatenate(p, axis=0) for p in parts]


def total_vector(vec, data_ways):
    if data_ways != 16:
        return lax.psum(vec, ("dp", "tensor"))
    vec = vec + lax.ppermute(vec, "tensor", [(0, 1), (1, 0)])
    for bit in (1, 2, 4, 8):
        vec = vec + lax.ppermute(vec, "dp", [(i, i ^ bit) for i in range(16)])
    return vec


def on_device(
    tokens,
    cotangent,
    seq_ids,
    block_slot,
    masters,
    left_stats,
    right_stats,
    left_roots,
    right_roots,
    vectors,
    vector_momentum,
):
    tensor_ways = lax.axis_size("tensor")
    tensor_index = lax.axis_index("tensor")
    data_ways = lax.axis_size("dp")
    data_index = lax.axis_index("dp")
    rows, dim = tokens.shape
    blk = masters.shape[-1]
    slot_count = masters.shape[1]
    width = dim // tensor_ways
    width_qkv = 3 * width
    hidden = FF // tensor_ways
    plan = Plan(data_ways, slot_count)

    codes = []
    for mat, (height, cols) in enumerate(((dim, width_qkv), (width, dim), (dim, hidden), (hidden, dim))):
        codes += [code_of(mat, r, c) for r in range(height // blk) for c in range(cols // blk)]
    codes = np.array(codes, np.int32)

    def coded(slots):
        hit = slots[:, None] == block_slot[None, :]
        return jnp.sum(jnp.where(hit, codes[None, :] + 1, 0), axis=1) - 1

    copies = masters[0].astype(BF)
    arrays = plan.gather(copies)
    table = coded(plan.positions(data_index, -1))
    where_to = coded(plan.positions(data_index, 1))
    my_slots = data_index * slot_count + jnp.arange(slot_count, dtype=jnp.int32)
    grad_scale = 1.0 / jnp.sqrt(jnp.float32(data_ways * rows))
    valid = jnp.where(coded(my_slots) >= 0, grad_scale, 0.0)

    gain_one = vectors[0:dim]
    bias_one = vectors[dim : 2 * dim]
    gain_two = vectors[2 * dim : 3 * dim]
    bias_two = vectors[3 * dim : 4 * dim]
    bias_qkv = lax.dynamic_slice_in_dim(vectors, 4 * dim + tensor_index * width_qkv, width_qkv)
    bias_attn = vectors[7 * dim : 8 * dim]
    bias_in = lax.dynamic_slice_in_dim(vectors, 8 * dim + tensor_index * hidden, hidden)
    bias_out = vectors[8 * dim + FF : 9 * dim + FF]
    places = jnp.arange(rows, dtype=jnp.int32)
    seq_first = jnp.concatenate([places[:1] == 0, seq_ids[1:] != seq_ids[:-1]])
    seq_start = lax.cummax(jnp.where(seq_first, places, 0), axis=0)
    position = (places - seq_start).astype(F32)
    half = ROT // 2
    inverse = 10000.0 ** (-(2.0 * jnp.arange(half, dtype=F32)) / ROT)
    angles = position[:, None] * inverse[None, :]
    cosine, sine = jnp.cos(angles), jnp.sin(angles)
    none = jnp.zeros((rows, half), F32)
    rest_one = jnp.ones((rows, HD - ROT), F32)
    rest_zero = jnp.zeros((rows, HD - ROT), F32)
    pair = 128 // HD
    tabs = (
        jnp.concatenate([cosine, cosine, rest_one] * pair, axis=1),
        jnp.concatenate([-sine, none, rest_zero] * pair, axis=1),
        jnp.concatenate([none, sine, rest_zero] * pair, axis=1),
    )
    single = (seq_ids[:1] == seq_ids[-1:]).astype(jnp.int32)
    tokens_f = tokens.astype(F32)
    row_mean = jnp.mean(tokens_f, axis=1, keepdims=True)
    centered = tokens_f - row_mean
    inv_std = lax.rsqrt(jnp.mean(centered * centered, axis=1, keepdims=True) + norm_eps)
    normed = centered * inv_std
    n1 = (normed * gain_one + bias_one).astype(BF)
    n2 = (normed * gain_two + bias_two).astype(BF)
    n1t, n2t, dyt = n1.T, n2.T, cotangent.T
    bias_grad_out = 0.5 * jnp.sum(cotangent.astype(F32), axis=0)

    ffn, dn2, grad_bias_in, sends = feed(
        table, where_to, arrays, n2, n2t, cotangent, dyt, bias_in[None], plan.send_shapes(blk)
    )
    q, k, v, da = project(table, arrays, n1, cotangent, bias_qkv[None], tabs, width)
    a, dq, dk, dv = attend(single, q, k, v, da, tabs)
    steps = rows // TILE
    order = (jnp.arange(steps, dtype=jnp.int32) + (1 - tensor_index) * (steps // 2)) % steps
    gains = jnp.stack([gain_one, gain_two])
    (own_mix, far_mix, own_in, far_in, sums, grad_bias_qkv), sends = close(
        table, where_to, order, arrays, sends,
        n1t, dq, dk, dv, a, dyt, tokens, row_mean, inv_std, dn2, ffn, gains,
    )
    swap = [(0, 1), (1, 0)]
    got_mix = lax.ppermute(far_mix, "tensor", swap)
    got_in = lax.ppermute(far_in, "tensor", swap)
    own_rows = rows // tensor_ways
    tokens_own = lax.dynamic_slice_in_dim(tokens, tensor_index * own_rows, own_rows, 0)
    cot_own = lax.dynamic_slice_in_dim(cotangent, tensor_index * own_rows, own_rows, 0)
    mixed = (
        tokens_own.astype(F32) + own_mix.astype(F32) + got_mix.astype(F32) + (bias_attn + bias_out)
    ).astype(BF)
    input_grad = cot_own.astype(F32) + own_in.astype(F32) + got_in.astype(F32)

    pieces = [
        sums[0],
        sums[1],
        sums[2],
        sums[3],
        lax.dynamic_update_slice_in_dim(
            jnp.zeros((3 * dim,), F32), grad_bias_qkv[0], tensor_index * width_qkv, 0
        ),
        bias_grad_out,
        lax.dynamic_update_slice_in_dim(jnp.zeros((FF,), F32), grad_bias_in[0], tensor_index * hidden, 0),
        bias_grad_out,
    ]
    vector_grad = total_vector(jnp.concatenate(pieces), data_ways) * grad_scale
    new_momentum = decay_vector * vector_momentum + (1.0 - decay_vector) * vector_grad
    new_vectors = vectors - rate_vector * new_momentum

    parts = plan.scatter(sends)
    grads, new_masters, new_left, new_right = own_update(
        valid, parts, masters[0], left_stats[0], right_stats[0], left_roots[0], right_roots[0]
    )
    return (
        mixed,
        input_grad,
        grads[None],
        new_masters[None],
        new_left[None],
        new_right[None],
        new_vectors,
        new_momentum,
    )


def solution(mesh):
    return jax.shard_map(
        on_device,
        mesh=mesh,
        in_specs=(
            P("dp", None),
            P("dp", None),
            P("dp"),
            P(),
            P("tensor", "dp", None, None),
            P("tensor", "dp", None, None),
            P("tensor", "dp", None, None),
            P("tensor", "dp", None, None),
            P("tensor", "dp", None, None),
            P(),
            P(),
        ),
        out_specs=(
            P(("dp", "tensor"), None),
            P(("dp", "tensor"), None),
            P("tensor", "dp", None, None),
            P("tensor", "dp", None, None),
            P("tensor", "dp", None, None),
            P("tensor", "dp", None, None),
            P(),
            P(),
        ),
        check_vma=False,
    )
```
